512 devices in a mesh: sub: 64 (over x, z), grp: 8 (over y, core).
Axes of the slice: x: 4, y: 4, z: 16, core: 2. Of those that a mesh axis runs over, the one named last changes fastest.
Arguments:
- rhs_jump: float32 [64, 8, 256, 256], P('sub', 'grp'), may hold values from -6 to 6
- incision: int32 [64, 8, 256], P('sub', 'grp'), may hold values 0 or 1
- precond: float32 [64, 8, 256], P('sub', 'grp'), may hold values from 0.5 to 2
- left_rows: int32 [64, 8, 256], P('sub', 'grp'), may hold values from 0 to 1151, as said below
- right_rows: int32 [64, 8, 256], P('sub', 'grp'), may hold values from 0 to 1151, as said below
- diag_inv: float32 [64, 8, 3, 384, 384], P('sub', 'grp'), as said below
- coupling: float32 [64, 8, 2, 384, 384], P('sub', 'grp'), may hold values from -0.09185587 to 0.09185587
- coarse_basis: float32 [64, 8, 3, 384, 128], P('sub', 'grp'), may hold values from -0.25 to 0.25
- coarse_inv: float32 [64, 128, 128], P('sub'), as said below
Outputs:
- multipliers: float32 [64, 8, 256, 256], P('sub', 'grp')
- residual: float32 [64, 8, 256, 256], P('sub', 'grp')
The draws below stay inside these ranges and needn't reach their ends.
Inputs may be any that keep to these rules, and one draw needn't show every extreme that they name: `left_rows`: for each subdomain, its 256 left rows and 256 right rows are 512 distinct interior rows. `right_rows`: see left_rows. `diag_inv`: every block is invertible. `coarse_inv`: every block is symmetric positive definite.
All inputs are finite; a program needn't handle non-finite values. No bound on the sum of `incision` on one device may be relied on, other than what follows from the above.
Results may differ from the reference program's by a relative error of at most 0.0003.
Values sent between devices are 32-bit elements; how exact they have to be, the bound alone decides.
No kernel may reach another device: no remote copies, remote signals or barrier semaphores. Data moves between devices by JAX's collectives and lax.ppermute only.
A program may use at most 64 MiB of HBM per device.

```python
import math
import jax
import jax.numpy as jnp
from jax import lax

BLK = 384
NB = 3
IFACE = 256
PRIMAL = 128
RHS = 256
ITERS = 3
SUBS = 64
GROUPS = 8


def interface_rows(key):
    base = jax.random.fold_in(key, 7)
    subkeys = jax.random.split(base, SUBS * GROUPS)

    def pick_rows(subkey):
        return jax.random.permutation(subkey, NB * BLK)[:2 * IFACE]
    picks = jax.vmap(pick_rows)(subkeys)
    return picks.reshape(SUBS, GROUPS, 2 * IFACE).astype(jnp.int32)


def draw_left_rows(key, part):
    return interface_rows(key)[:, :, :IFACE]


def draw_right_rows(key, part):
    return interface_rows(key)[:, :, IFACE:]


def draw_diag_inv(key, part):
    first, second = jax.random.split(jax.random.fold_in(key, 11))
    scales = jnp.exp(jax.random.uniform(first, (SUBS, GROUPS, NB, BLK), jnp.float32, 0.0, 0.693))
    noise = 0.25 * jax.random.normal(second, (SUBS, GROUPS, NB, BLK, BLK), jnp.float32) / BLK ** 0.5
    ident = jnp.eye(BLK, dtype=jnp.float32)
    return noise + scales[..., None] * ident


def draw_coarse_inv(key, part):
    first, second = jax.random.split(jax.random.fold_in(key, 13))
    factor = jax.random.normal(first, (SUBS, PRIMAL, PRIMAL), jnp.float32)
    diagonal = jnp.exp(jax.random.uniform(second, (SUBS, PRIMAL), jnp.float32, -0.693, 0.693))
    gram = jnp.einsum('spk,sqk->spq', factor, factor) * (0.5 / PRIMAL)
    return gram + diagonal[..., None] * jnp.eye(PRIMAL, dtype=jnp.float32)


def with_ends(values, key, least, high):
    index_at = [jax.random.randint(jax.random.fold_in(key, axis), (), 0, length) for axis, length in enumerate(values.shape)]
    widest = values.shape.index(max(values.shape))
    next_to = index_at[:widest] + [(index_at[widest] + 1) % values.shape[widest]] + index_at[widest + 1:]
    return values.at[tuple(index_at)].set(least).at[tuple(next_to)].set(high)


def block_scale(key, dims, cuts, least, high):
    level = 1.0
    for axis_at, blocks in cuts:
        draws = jax.random.uniform(jax.random.fold_in(jax.random.fold_in(key, 6), axis_at), (blocks,), jnp.float32, least / len(cuts), high / len(cuts))
        level = level * jnp.repeat(jnp.exp(draws), dims[axis_at] // blocks).reshape((-1,) + (1,) * (len(dims) - 1 - axis_at))
    return level


def bell_draw(key, shape, deviation, limit, shards=(), held_as=jnp.bfloat16):
    loudness = block_scale(key, shape, shards, -0.22, 0.18) if shards else 1.0
    entries = jax.random.normal(key, shape, jnp.float32) * deviation * loudness
    return jnp.minimum(jnp.maximum(entries, -limit), limit).astype(held_as)


def setup_inputs(seed: int = 0) -> dict:
    key_list = jax.random.split(jax.random.key(seed), 10)
    rhs_jump = bell_draw(key_list[0], (SUBS, GROUPS, IFACE, RHS), 1.0, 6.0, ((0, 64), (1, 8)), jnp.float32)
    incision = with_ends((jax.random.randint(key_list[1], (SUBS, GROUPS, IFACE), 0, 8) < 7).astype(jnp.int32), jax.random.fold_in(key_list[1], 1), 0, 1)
    precond = jnp.clip(jnp.exp(math.log(2.0) - 1.3862944 * jax.random.uniform(key_list[2], (SUBS, GROUPS, IFACE), jnp.float32) ** block_scale(key_list[2], (SUBS, GROUPS, IFACE), ((0, 64), (1, 8)), -0.2, 0.2)), 0.5, 2.0)
    left_rows = draw_left_rows(jax.random.fold_in(key_list[9], 71), 0)
    right_rows = draw_right_rows(jax.random.fold_in(key_list[9], 71), 0)
    diag_inv = draw_diag_inv(jax.random.fold_in(key_list[9], 71), 0)
    coupling = bell_draw(key_list[6], (SUBS, GROUPS, NB - 1, BLK, BLK), (0.3 / BLK ** 0.5), 0.09185587, ((0, 64), (1, 8)), jnp.float32)
    coarse_basis = bell_draw(key_list[7], (SUBS, GROUPS, NB, BLK, PRIMAL), (2 * IFACE) ** -0.5, 0.25, ((0, 64), (1, 8)), jnp.float32)
    coarse_inv = draw_coarse_inv(jax.random.fold_in(key_list[9], 71), 0)
    return {"rhs_jump": rhs_jump, "incision": incision, "precond": precond, "left_rows": left_rows, "right_rows": right_rows, "diag_inv": diag_inv, "coupling": coupling, "coarse_basis": coarse_basis, "coarse_inv": coarse_inv}


HIGH = lax.Precision.HIGHEST


def banded(dinv, coup, load):
    forward = []
    for block in range(NB):
        rhs_now = load[:, block]
        if block > 0:
            rhs_now = rhs_now - jnp.einsum("qab,qbr->qar", coup[:, block - 1], forward[-1], precision=HIGH)
        forward.append(jnp.einsum("qab,qbr->qar", dinv[:, block], rhs_now, precision=HIGH))
    backward = [None] * NB
    for block in range(NB - 1, -1, -1):
        rhs_now = forward[block]
        if block < NB - 1:
            rhs_now = rhs_now - jnp.einsum("qba,qbr->qar", coup[:, block], backward[block + 1], precision=HIGH)
        backward[block] = jnp.einsum("qba,qbr->qar", dinv[:, block], rhs_now, precision=HIGH)
    return jnp.stack(backward, axis=1)


def build_load(rrow, lrow, own, left):
    order = NB * BLK
    zeros = jnp.zeros((order, own.shape[1]), jnp.float32)
    return zeros.at[rrow].add(own).at[lrow].add(-left)


def reference(rhs_jump, incision, precond, left_rows, right_rows, diag_inv, coupling, coarse_basis, coarse_inv):
    count = SUBS * GROUPS
    order = NB * BLK
    cut = incision.astype(jnp.float32)[..., None]
    scaling = precond[..., None]
    lflat = left_rows.reshape(count, IFACE)
    rflat = right_rows.reshape(count, IFACE)
    dinv = diag_inv.reshape(count, NB, BLK, BLK)
    coup = coupling.reshape(count, NB - 1, BLK, BLK)
    basis = coarse_basis.reshape(count, order, PRIMAL)

    def apply(direc):
        left = jnp.roll(direc, 1, axis=0)
        load = jax.vmap(build_load)(rflat, lflat, direc.reshape(count, IFACE, RHS), left.reshape(count, IFACE, RHS))
        interior = banded(dinv, coup, load.reshape(count, NB, BLK, RHS)).reshape(count, order, RHS)
        wsum = jnp.einsum("qnp,qnr->qpr", basis, load, precision=HIGH).reshape(SUBS, GROUPS, PRIMAL, RHS).sum(axis=1)
        coarse = jnp.einsum("spk,skr->spr", coarse_inv, wsum, precision=HIGH)
        coarse_all = jnp.broadcast_to(coarse[:, None], (SUBS, GROUPS, PRIMAL, RHS)).reshape(count, PRIMAL, RHS)
        disp = interior + jnp.einsum("qnp,qpr->qnr", basis, coarse_all, precision=HIGH)
        yright = jax.vmap(lambda v, i: v[i])(disp, rflat).reshape(SUBS, GROUPS, IFACE, RHS)
        yleft = jax.vmap(lambda v, i: v[i])(disp, lflat).reshape(SUBS, GROUPS, IFACE, RHS)
        return cut * (yright - jnp.roll(yleft, -1, axis=0))

    def total(a, b):
        return jnp.sum(a * b, axis=(0, 1, 2))

    multipliers = jnp.zeros_like(rhs_jump)
    residual = cut * rhs_jump
    zvec = scaling * residual
    direc = zvec
    rz_now = total(residual, zvec)
    for step in range(ITERS):
        image = apply(direc)
        alpha = rz_now / total(direc, image)
        multipliers = multipliers + alpha * direc
        residual = residual - alpha * image
        if step + 1 < ITERS:
            zvec = scaling * residual
            rz_new = total(residual, zvec)
            direc = zvec + (rz_new / rz_now) * direc
            rz_now = rz_new
    return multipliers, residual
```

```python
import jax
import jax.numpy as jnp
from jax import lax
from jax.sharding import PartitionSpec as P


ITERS = 3
HIGH = lax.Precision.HIGH
FULL = lax.Precision.HIGHEST


def passed_along(shard, axis, by):
    peers = lax.axis_size(axis)
    return lax.ppermute(shard, axis, [(i, (i + by) % peers) for i in range(peers)])


def exchanged(parts, axis):
    return lax.all_to_all(parts, axis, 0, 0)


def spread(part, axis):
    peers = lax.axis_size(axis)
    return exchanged(jnp.broadcast_to(part[None], (peers,) + part.shape), axis)


def grp_sum(value):
    peers = lax.axis_size("grp")
    rows, width = value.shape
    part = jnp.sum(exchanged(value.reshape(peers, rows // peers, width), "grp"), axis=0)
    return spread(part, "grp").reshape(rows, width)


def conjugate(gram):
    def inner(first, second):
        total = 0.0
        for i, a in enumerate(first):
            for j, b in enumerate(second):
                if a is not None and b is not None:
                    total = total + a * b * gram[min(i, j), max(i, j)]
        return total

    def plus(first, factor, second):
        out = []
        for i in range(max(len(first), len(second))):
            a = first[i] if i < len(first) else None
            b = second[i] if i < len(second) else None
            if b is None:
                out.append(a)
            elif a is None:
                out.append(factor * b)
            else:
                out.append(a + factor * b)
        return out

    one = jnp.ones_like(gram[0, 0])
    resid, direc, mult = [one], [one], []
    rz_now = gram[0, 0]
    for step in range(ITERS):
        image = [None] + direc
        alpha = rz_now / inner(direc, image)
        mult = plus(mult, alpha, direc)
        resid = plus(resid, -alpha, image)
        if step + 1 < ITERS:
            rz_new = inner(resid, resid)
            direc = plus(resid, rz_new / rz_now, direc)
            rz_now = rz_new
    return mult, resid


def local(
    rhs_jump, incision, precond, left_rows, right_rows, diag_inv, coupling, coarse_basis, coarse_inv
):
    rhs = rhs_jump[0, 0]
    iface, width = rhs.shape
    cut = incision[0, 0].astype(jnp.float32)
    weight = precond[0, 0] * cut
    first = weight[:, None] * rhs
    sent = passed_along(jnp.concatenate([first, jnp.broadcast_to(weight[None], (8, iface))]), "sub", 1)
    first_left = sent[:iface]
    weight_left = sent[iface]

    dinv = diag_inv[0, 0]
    coup = coupling[0, 0]
    nblk, blk = dinv.shape[0], dinv.shape[1]
    basis = coarse_basis[0, 0]
    rows = jnp.concatenate([right_rows[0, 0], left_rows[0, 0]])
    picks = [
        (lax.broadcasted_iota(jnp.int32, (blk, 2 * iface), 0) + k * blk == rows[None]).astype(jnp.float32)
        for k in range(nblk)
    ]
    sweeps = []
    for k in range(nblk):
        now = picks[k]
        if k > 0:
            now = now - jnp.dot(coup[k - 1], sweeps[-1], precision=HIGH)
        sweeps.append(jnp.dot(dinv[k], now, precision=HIGH))
    sweep = jnp.concatenate(sweeps, axis=0)
    schur = lax.dot_general(sweep, sweep, (((0,), (0,)), ((), ())), precision=HIGH)
    pick = jnp.concatenate(picks, axis=0)
    modes = lax.dot_general(pick, basis.reshape(nblk * blk, -1), (((0,), (0,)), ((), ())), precision=FULL)
    probe = lax.dot_general(coarse_inv[0], modes, (((1,), (1,)), ((), ())), precision=FULL)

    scale = jnp.concatenate([weight, -weight_left])[:, None]
    peers = lax.axis_size("grp")
    primal = modes.shape[1]
    deal = primal // peers
    loads = [jnp.concatenate([first, -first_left])]
    vectors = [cut[:, None] * rhs]
    disps = []
    for step in range(ITERS - 1):
        load = loads[-1]
        coarse = grp_sum(jnp.dot(probe, load, precision=FULL))
        disp = jnp.dot(schur, load, precision=FULL) + jnp.dot(modes, coarse, precision=FULL)
        disps.append(disp)
        right, left = disp[:iface], disp[iface:]
        from_next = passed_along(left, "sub", -1)
        from_prev = passed_along(right, "sub", 1)
        early = []
        if step == 1:
            early = [
                jnp.sum(first * rhs, axis=0),
                jnp.sum(loads[0] * disps[0], axis=0),
                jnp.sum(loads[1] * disps[0], axis=0),
                jnp.sum(loads[1] * disps[1], axis=0),
            ]
        from_next, from_prev, *early = lax.optimization_barrier((from_next, from_prev, *early))
        vectors.append(cut[:, None] * (right - from_next))
        loads.append(scale * jnp.concatenate([right - from_next, from_prev - left]))

    load = loads[-1]
    both = jnp.concatenate(
        [probe.reshape(peers, deal, -1), modes.T.reshape(peers, deal, -1)], axis=1
    ).reshape(2 * primal, -1)
    parts = jnp.dot(both, load, precision=FULL).reshape(peers, 2 * deal, width)
    solved = jnp.dot(schur, load, precision=FULL)
    late = [jnp.sum(load * disps[1], axis=0), jnp.sum(load * solved, axis=0)]
    got, *late = lax.optimization_barrier((exchanged(parts, "grp"), *late))
    part = jnp.sum(got, axis=0)
    moments = early + [late[0], late[1] + jnp.sum(part[:deal] * part[deal:], axis=0)]
    moments = jnp.stack(moments + [jnp.zeros_like(moments[0])] * (peers - len(moments)))
    gathered = spread(jnp.concatenate([part[:deal], moments]), "grp")
    coarse = gathered[:, :deal].reshape(primal, width)
    disp = solved + jnp.dot(modes, coarse, precision=FULL)
    right, left = disp[:iface], disp[iface:]
    from_next = passed_along(left, "sub", -1)
    mine = lax.broadcasted_iota(jnp.int32, (peers, 1), 0) == lax.axis_index("grp")
    owned = jnp.sum(jnp.where(mine, jnp.sum(gathered[:, deal:], axis=0), 0.0), axis=0)
    owned = jnp.broadcast_to(owned.reshape(1, -1, 128), (lax.axis_size("sub"), width // 128, 128))
    owned = exchanged(owned, "sub")
    sums = spread(jnp.sum(owned, axis=0), "grp").reshape(peers, width)
    vectors.append(cut[:, None] * (right - from_next))
    gram = {(i, j): sums[i + j] for i in range(ITERS) for j in range(i, ITERS + 1)}
    mult, resid = conjugate(gram)
    multipliers = sum(c[None] * load[:iface] for c, load in zip(mult, loads))
    residual = sum(c[None] * vector for c, vector in zip(resid, vectors))
    return (multipliers[None, None], residual[None, None])


def solution(mesh):
    placed = (
        P("sub", "grp", None, None),
        P("sub", "grp", None),
        P("sub", "grp", None),
        P("sub", "grp", None),
        P("sub", "grp", None),
        P("sub", "grp", None, None, None),
        P("sub", "grp", None, None, None),
        P("sub", "grp", None, None, None),
        P("sub", None, None),
    )

    return jax.shard_map(
        local,
        mesh=mesh,
        in_specs=placed,
        out_specs=(P("sub", "grp", None, None), P("sub", "grp", None, None)),
        check_vma=False,
    )
```

```python
import functools

import jax
import jax.numpy as jnp
from jax import lax
from jax.experimental import pallas as pl
from jax.experimental.pallas import tpu as pltpu
from jax.sharding import PartitionSpec as P


ITERS = 3
HIGH = lax.Precision.HIGH
FULL = lax.Precision.HIGHEST
F32 = jnp.float32


def passed_along(shard, axis, by):
    peers = lax.axis_size(axis)
    return lax.ppermute(shard, axis, [(i, (i + by) % peers) for i in range(peers)])


def exchanged(parts, axis, groups=None):
    return lax.all_to_all(parts, axis, 0, 0, axis_index_groups=groups)


def fused(body, *shapes, held=(), kept=(), room=()):
    out = [jax.ShapeDtypeStruct(shape, F32) for shape in shapes]
    near = pl.BlockSpec(memory_space=pltpu.VMEM)
    far = pl.BlockSpec(memory_space=pltpu.HBM)

    def call(*args):
        return pl.pallas_call(
            body,
            out_shape=out,
            in_specs=[far if i in held else near for i in range(len(args))],
            out_specs=[far if i in kept else near for i in range(len(out))],
            scratch_shapes=[pltpu.VMEM(shape, dtype) for shape, dtype in room]
            + ([pltpu.SemaphoreType.DMA((len(room),))] if room else []),
            compiler_params=pltpu.CompilerParams(vmem_limit_bytes=8 << 20),
        )(*args)

    return call


def copies(sources, targets, sems):
    made = [pltpu.make_async_copy(s, t, sems.at[i]) for i, (s, t) in enumerate(zip(sources, targets))]
    for copy in made:
        copy.start()
    return made


def product(first, second):
    return jnp.dot(first, second, precision=FULL, preferred_element_type=F32)


def column(row):
    return jnp.transpose(jnp.broadcast_to(row, (128, row.shape[1])))


def times(col, value):
    return jnp.concatenate(
        [col * value[:, i:i + 128] for i in range(0, value.shape[1], 128)], axis=1
    )


def begin(cut, pre, weights, cuts):
    keep = cut[...].astype(F32)
    cuts[...] = column(keep)
    weights[...] = column(pre[...] * keep)


def halves(total, mine, away):
    half = mine.shape[0]
    odd = lax.axis_index("grp") % 2 == 1
    mine[...] = jnp.where(odd, total[half:], total[:half])
    away[...] = jnp.where(odd, total[:half], total[half:])


def paired(mine, got, out):
    total = mine[...] + got[...]
    for i in range(out.shape[0]):
        out[i] = total


def summed(got, out):
    total = got[0]
    for i in range(1, got.shape[0]):
        total = total + got[i]
    out[...] = total


def displace_pair(solved, modes, mine, got, right, left):
    iface = right.shape[0]
    odd = lax.axis_index("grp") % 2 == 1
    top, low = jnp.where(odd, got[...], mine[...]), jnp.where(odd, mine[...], got[...])
    value = solved[...] + product(modes[...], jnp.concatenate([top, low], axis=0))
    right[...] = value[:iface]
    left[...] = value[iface:]


def enter(rhs, got, got_weight, weights, probe, load_far, scale, mine, away, load, sems):
    iface = weights.shape[0]
    side = -column(got_weight[pl.ds(0, 1), :])
    scale[pl.ds(0, iface), :] = weights[...]
    scale[pl.ds(iface, iface), :] = side
    load[pl.ds(0, iface), :] = times(weights[...], rhs[...])
    load[pl.ds(iface, iface), :] = times(side, got[...])
    (made,) = copies((load,), (load_far,), sems)
    halves(product(probe[...], load[...]), mine, away)
    made.wait()


def again(
    right, left, from_next, from_prev, scale, probe, load_far, jump_far, mine, away, load, jump, sems
):
    iface = right.shape[0]
    value = right[...] - from_next[...]
    jump[...] = value
    load[pl.ds(0, iface), :] = times(scale[pl.ds(0, iface), :], value)
    load[pl.ds(iface, iface), :] = times(scale[pl.ds(iface, iface), :], from_prev[...] - left[...])
    made = copies((load, jump), (load_far, jump_far), sems)
    halves(product(probe[...], load[...]), mine, away)
    for copy in made:
        copy.wait()


def again_last(
    right, left, from_next, from_prev, scale, probe, modes, load_far, jump_far, parts,
    load, jump, sems
):
    iface = right.shape[0]
    deal = parts.shape[1] // 2
    value = right[...] - from_next[...]
    jump[...] = value
    load[pl.ds(0, iface), :] = times(scale[pl.ds(0, iface), :], value)
    load[pl.ds(iface, iface), :] = times(scale[pl.ds(iface, iface), :], from_prev[...] - left[...])
    made = copies((load, jump), (load_far, jump_far), sems)
    coarse = product(probe[...], load[...])
    raw = product(modes[...].T, load[...])
    for i in range(parts.shape[0]):
        parts[i, pl.ds(0, deal), :] = coarse[i * deal:(i + 1) * deal]
        parts[i, pl.ds(deal, deal), :] = raw[i * deal:(i + 1) * deal]
    for copy in made:
        copy.wait()


def solve(schur, load_far, solved, load, sems):
    (made,) = copies((load_far,), (load,), sems)
    made.wait()
    solved[...] = product(schur[...], load[...])


def solve_last(
    schur, scale, load_far, rhs_far, first_far, second_far, solved, moments,
    load, rhs, first, second, sems
):
    made = copies((load_far, rhs_far, first_far, second_far), (load, rhs, first, second), sems)
    iface = rhs.shape[0]
    made[0].wait()
    value = product(schur[...], load[...])
    solved[...] = value
    for copy in made[1:]:
        copy.wait()
    u = [rhs[...], first[...], second[...]]
    p = [times(scale[pl.ds(0, iface), :], value) for value in u]
    rows = [jnp.sum(p[(k + 1) // 2] * u[k // 2], axis=0, keepdims=True) for k in range(5)]
    rows.append(jnp.sum(load[...] * value, axis=0, keepdims=True))
    moments[...] = jnp.zeros_like(moments)
    for k, row in enumerate(rows):
        moments[pl.ds(k, 1), :] = row


def added(got, out):
    total = got[0]
    for i in range(1, got.shape[0]):
        total = total + got[i]
    for i in range(out.shape[0]):
        out[i] = total


def added_last(got, moments, out):
    deal = got.shape[1] // 2
    total = got[0]
    for i in range(1, got.shape[0]):
        total = total + got[i]
    coarse, energy = total[:deal], total[:deal] * total[deal:]
    rows = moments[...]
    energy = jnp.sum(energy, axis=0, keepdims=True)
    which = lax.broadcasted_iota(jnp.int32, rows.shape, 0) == 5
    rows = rows + jnp.where(which, energy, 0.0)
    for i in range(out.shape[0]):
        out[i, pl.ds(0, deal), :] = coarse
        out[i, pl.ds(deal, rows.shape[0]), :] = rows


def displace(deal, solved, modes, gathered, right, left):
    iface = right.shape[0]
    coarse = jnp.concatenate([gathered[i, pl.ds(0, deal), :] for i in range(gathered.shape[0])], axis=0)
    value = solved[...] + product(modes[...], coarse)
    right[...] = value[:iface]
    left[...] = value[iface:]


def tally(deal, gathered, out):
    rows = gathered[0, pl.ds(deal, 8), :]
    for i in range(1, gathered.shape[0]):
        rows = rows + gathered[i, pl.ds(deal, 8), :]
    for i in range(out.shape[0]):
        out[i] = rows


def conjugate(moment):
    def inner(first, second):
        total = 0.0
        for i, a in enumerate(first):
            for j, b in enumerate(second):
                if a is not None and b is not None:
                    total = total + a * b * moment[i + j]
        return total

    def plus(first, factor, second):
        out = []
        for i in range(max(len(first), len(second))):
            a = first[i] if i < len(first) else None
            b = second[i] if i < len(second) else None
            if b is None:
                out.append(a)
            elif a is None:
                out.append(factor * b)
            else:
                out.append(a + factor * b)
        return out

    one = jnp.ones_like(moment[0])
    resid, direc, mult = [one], [one], []
    rz_now = moment[0]
    for step in range(ITERS):
        image = [None] + direc
        alpha = rz_now / inner(direc, image)
        mult = plus(mult, alpha, direc)
        resid = plus(resid, -alpha, image)
        if step + 1 < ITERS:
            rz_new = inner(resid, resid)
            direc = plus(resid, rz_new / rz_now, direc)
            rz_now = rz_new
    return mult, resid


def finish(
    sums, right, from_next, scale, cuts, rhs_far, first_far, second_far, mult, resid,
    rhs, first, second, sems
):
    made = copies((rhs_far, first_far, second_far), (rhs, first, second), sems)
    iface = right.shape[0]
    total = sums[0]
    for i in range(1, sums.shape[0]):
        total = total + sums[i]
    mults, resids = conjugate([total[i:i + 1] for i in range(2 * ITERS)])
    for copy in made:
        copy.wait()
    u = [rhs[...], first[...], second[...], right[...] - from_next[...]]
    mult[...] = times(scale[pl.ds(0, iface), :], sum(c * v for c, v in zip(mults, u)))
    resid[...] = times(cuts[...], sum(c * v for c, v in zip(resids, u)))


def local(
    rhs_jump, incision, precond, left_rows, right_rows, diag_inv, coupling, coarse_basis, coarse_inv
):
    rhs = rhs_jump[0, 0]
    iface, width = rhs.shape
    peers = lax.axis_size("grp")
    plane, tall = (iface, width), (2 * iface, width)
    near, whole = (plane, F32), (tall, F32)
    got = passed_along(rhs, "sub", 1)
    weight = precond[0] * incision[0].astype(F32)
    got_weight = passed_along(jnp.broadcast_to(weight, (8, iface)), "sub", 1)
    weights, cuts = fused(begin, (iface, 128), (iface, 128))(incision[0], precond[0])

    dinv = diag_inv[0, 0]
    coup = coupling[0, 0]
    nblk, blk = dinv.shape[0], dinv.shape[1]
    basis = coarse_basis[0, 0]
    rows = jnp.concatenate([right_rows[0, 0], left_rows[0, 0]])
    picks = [
        (lax.broadcasted_iota(jnp.int32, (blk, 2 * iface), 0) + k * blk == rows[None]).astype(F32)
        for k in range(nblk)
    ]
    sweeps = []
    for k in range(nblk):
        now = picks[k]
        if k > 0:
            now = now - jnp.dot(coup[k - 1], sweeps[-1], precision=HIGH)
        sweeps.append(jnp.dot(dinv[k], now, precision=HIGH))
    sweep = jnp.concatenate(sweeps, axis=0)
    schur = lax.dot_general(sweep, sweep, (((0,), (0,)), ((), ())), precision=HIGH)
    pick = jnp.concatenate(picks, axis=0)
    modes = lax.dot_general(pick, basis.reshape(nblk * blk, -1), (((0,), (0,)), ((), ())), precision=FULL)
    probe = lax.dot_general(coarse_inv[0], modes, (((1,), (1,)), ((), ())), precision=FULL)
    primal = modes.shape[1]
    deal = primal // peers
    pair = (primal // 2, width)
    chips = [[i for i in range(peers) if i % 2 == core] for core in range(2)]
    swap = [(i, i ^ 1) for i in range(peers)]
    load, scale, mine, away = fused(
        enter, tall, (2 * iface, 128), pair, pair, kept=(0,), room=[whole]
    )(rhs, got, got_weight, weights, probe)
    jumps = [rhs]
    for step in range(ITERS - 1):
        (both,) = fused(paired, (peers // 2,) + pair)(mine, lax.ppermute(away, "grp", swap))
        both = exchanged(both, "grp", chips)
        (solved,) = fused(solve, tall, held=(1,), room=[whole])(schur, load)
        (mine,) = fused(summed, pair)(both)
        right, left = fused(displace_pair, plane, plane)(
            solved, modes, mine, lax.ppermute(mine, "grp", swap)
        )
        from_next = passed_along(left, "sub", -1)
        from_prev = passed_along(right, "sub", 1)
        sides = (right, left, from_next, from_prev, scale)
        if step + 2 == ITERS:
            load, jump, parts = fused(
                again_last, tall, plane, (peers, 2 * deal, width),
                kept=(0, 1), room=[whole, near],
            )(*sides, probe, modes)
        else:
            load, jump, mine, away = fused(
                again, tall, plane, pair, pair, kept=(0, 1), room=[whole, near]
            )(*sides, probe)
        jumps.append(jump)
    got = exchanged(parts, "grp")
    solved, moments = fused(
        solve_last, tall, (peers, width), held=(2, 3, 4, 5),
        room=[whole, near, near, near],
    )(schur, scale, load, *jumps)
    (spread,) = fused(added_last, (peers, deal + peers, width))(got, moments)
    gathered = exchanged(spread, "grp")

    size = lax.axis_size("sub")
    run = size // 4
    runs = [[i * run + j for j in range(run)] for i in range(4)]
    across = [[i * run + j for i in range(4)] for j in range(run)]
    (sums,) = fused(functools.partial(tally, deal), (run, 8, width))(gathered)
    sums = exchanged(sums, "sub", runs)
    right, left = fused(functools.partial(displace, deal), plane, plane)(solved, modes, gathered)
    from_next = passed_along(left, "sub", -1)
    (sums,) = fused(added, (4, 8, width))(sums)
    sums = exchanged(sums, "sub", across)
    multipliers, residual = fused(
        finish, plane, plane, held=(5, 6, 7), room=[near, near, near]
    )(sums, right, from_next, scale, cuts, *jumps)
    return (multipliers[None, None], residual[None, None])


def solution(mesh):
    placed = (
        P("sub", "grp", None, None),
        P("sub", "grp", None),
        P("sub", "grp", None),
        P("sub", "grp", None),
        P("sub", "grp", None),
        P("sub", "grp", None, None, None),
        P("sub", "grp", None, None, None),
        P("sub", "grp", None, None, None),
        P("sub", None, None),
    )

    return jax.shard_map(
        local,
        mesh=mesh,
        in_specs=placed,
        out_specs=(P("sub", "grp", None, None), P("sub", "grp", None, None)),
        check_vma=False,
    )
```

```python
import functools

import jax
import jax.numpy as jnp
from jax import lax
from jax.experimental import pallas as pl
from jax.experimental.pallas import tpu as pltpu
from jax.sharding import PartitionSpec as P


ITERS = 3
HIGH = lax.Precision.HIGH
FULL = lax.Precision.HIGHEST
F32 = jnp.float32


def passed_along(shard, axis, by):
    peers = lax.axis_size(axis)
    return lax.ppermute(shard, axis, [(i, (i + by) % peers) for i in range(peers)])


def exchanged(parts, axis, groups=None):
    return lax.all_to_all(parts, axis, 0, 0, axis_index_groups=groups)


def fused(body, *shapes, held=(), kept=(), room=()):
    out = [jax.ShapeDtypeStruct(shape, F32) for shape in shapes]
    near = pl.BlockSpec(memory_space=pltpu.VMEM)
    far = pl.BlockSpec(memory_space=pltpu.HBM)

    def call(*args):
        return pl.pallas_call(
            body,
            out_shape=out,
            in_specs=[far if i in held else near for i in range(len(args))],
            out_specs=[far if i in kept else near for i in range(len(out))],
            scratch_shapes=[pltpu.VMEM(shape, dtype) for shape, dtype in room]
            + ([pltpu.SemaphoreType.DMA((len(room),))] if room else []),
            compiler_params=pltpu.CompilerParams(vmem_limit_bytes=8 << 20),
        )(*args)

    return call


def copies(sources, targets, sems):
    made = [pltpu.make_async_copy(s, t, sems.at[i]) for i, (s, t) in enumerate(zip(sources, targets))]
    for copy in made:
        copy.start()
    return made


def product(first, second):
    return jnp.dot(first, second, precision=FULL, preferred_element_type=F32)


def column(row):
    return jnp.transpose(jnp.broadcast_to(row, (128, row.shape[1])))


def times(col, value):
    return jnp.concatenate(
        [col * value[:, i:i + 128] for i in range(0, value.shape[1], 128)], axis=1
    )


def begin(cut, pre, weights, cuts):
    keep = cut[...].astype(F32)
    cuts[...] = column(keep)
    weights[...] = column(pre[...] * keep)


def halves(total, mine, away):
    half = mine.shape[0]
    odd = lax.axis_index("grp") % 2 == 1
    mine[...] = jnp.where(odd, total[half:], total[:half])
    away[...] = jnp.where(odd, total[:half], total[half:])


def paired(mine, got, out):
    total = mine[...] + got[...]
    for i in range(out.shape[0]):
        out[i] = total


def summed(got, out):
    total = got[0]
    for i in range(1, got.shape[0]):
        total = total + got[i]
    out[...] = total


def displace_pair(solved, modes, mine, got, right, left):
    iface = right.shape[0]
    odd = lax.axis_index("grp") % 2 == 1
    top, low = jnp.where(odd, got[...], mine[...]), jnp.where(odd, mine[...], got[...])
    value = solved[...] + product(modes[...], jnp.concatenate([top, low], axis=0))
    right[...] = value[:iface]
    left[...] = value[iface:]


def enter(rhs, got, got_weight, weights, probe, load_far, scale, mine, away, load, sems):
    iface = weights.shape[0]
    side = -column(got_weight[pl.ds(0, 1), :])
    scale[pl.ds(0, iface), :] = weights[...]
    scale[pl.ds(iface, iface), :] = side
    load[pl.ds(0, iface), :] = times(weights[...], rhs[...])
    load[pl.ds(iface, iface), :] = times(side, got[...])
    (made,) = copies((load,), (load_far,), sems)
    halves(product(probe[...], load[...]), mine, away)
    made.wait()


def again(
    right, left, from_next, from_prev, scale, probe, load_far, jump_far, mine, away, load, jump, sems
):
    iface = right.shape[0]
    value = right[...] - from_next[...]
    jump[...] = value
    load[pl.ds(0, iface), :] = times(scale[pl.ds(0, iface), :], value)
    load[pl.ds(iface, iface), :] = times(scale[pl.ds(iface, iface), :], from_prev[...] - left[...])
    made = copies((load, jump), (load_far, jump_far), sems)
    halves(product(probe[...], load[...]), mine, away)
    for copy in made:
        copy.wait()


def again_last(
    right, left, from_next, from_prev, scale, probe, modes, load_far, jump_far, parts,
    load, jump, sems
):
    iface = right.shape[0]
    deal = parts.shape[1] // 2
    value = right[...] - from_next[...]
    jump[...] = value
    load[pl.ds(0, iface), :] = times(scale[pl.ds(0, iface), :], value)
    load[pl.ds(iface, iface), :] = times(scale[pl.ds(iface, iface), :], from_prev[...] - left[...])
    made = copies((load, jump), (load_far, jump_far), sems)
    coarse = product(probe[...], load[...])
    raw = product(modes[...].T, load[...])
    for i in range(parts.shape[0]):
        parts[i, pl.ds(0, deal), :] = coarse[i * deal:(i + 1) * deal]
        parts[i, pl.ds(deal, deal), :] = raw[i * deal:(i + 1) * deal]
    for copy in made:
        copy.wait()


def solve(schur, load_far, solved, load, sems):
    (made,) = copies((load_far,), (load,), sems)
    made.wait()
    solved[...] = product(schur[...], load[...])


def solve_last(
    schur, scale, load_far, rhs_far, first_far, second_far, solved, moments,
    load, rhs, first, second, sems
):
    made = copies((load_far, rhs_far, first_far, second_far), (load, rhs, first, second), sems)
    iface = rhs.shape[0]
    made[0].wait()
    value = product(schur[...], load[...])
    solved[...] = value
    for copy in made[1:]:
        copy.wait()
    u = [rhs[...], first[...], second[...]]
    p = [times(scale[pl.ds(0, iface), :], value) for value in u]
    rows = [jnp.sum(p[(k + 1) // 2] * u[k // 2], axis=0, keepdims=True) for k in range(5)]
    rows.append(jnp.sum(load[...] * value, axis=0, keepdims=True))
    moments[...] = jnp.zeros_like(moments)
    for k, row in enumerate(rows):
        moments[pl.ds(k, 1), :] = row


def added(got, out):
    total = got[0]
    for i in range(1, got.shape[0]):
        total = total + got[i]
    for i in range(out.shape[0]):
        out[i] = total


def added_last(got, moments, out):
    deal = got.shape[1] // 2
    total = got[0]
    for i in range(1, got.shape[0]):
        total = total + got[i]
    coarse, energy = total[:deal], total[:deal] * total[deal:]
    rows = moments[...]
    energy = jnp.sum(energy, axis=0, keepdims=True)
    which = lax.broadcasted_iota(jnp.int32, rows.shape, 0) == 5
    rows = rows + jnp.where(which, energy, 0.0)
    for i in range(out.shape[0]):
        out[i, pl.ds(0, deal), :] = coarse
        out[i, pl.ds(deal, rows.shape[0]), :] = rows


def displace(deal, solved, modes, gathered, right, left):
    iface = right.shape[0]
    coarse = jnp.concatenate([gathered[i, pl.ds(0, deal), :] for i in range(gathered.shape[0])], axis=0)
    value = solved[...] + product(modes[...], coarse)
    right[...] = value[:iface]
    left[...] = value[iface:]


def tally(deal, gathered, out):
    rows = gathered[0, pl.ds(deal, 8), :]
    for i in range(1, gathered.shape[0]):
        rows = rows + gathered[i, pl.ds(deal, 8), :]
    for i in range(out.shape[0]):
        out[i] = rows


def conjugate(moment):
    def inner(first, second):
        total = 0.0
        for i, a in enumerate(first):
            for j, b in enumerate(second):
                if a is not None and b is not None:
                    total = total + a * b * moment[i + j]
        return total

    def plus(first, factor, second):
        out = []
        for i in range(max(len(first), len(second))):
            a = first[i] if i < len(first) else None
            b = second[i] if i < len(second) else None
            if b is None:
                out.append(a)
            elif a is None:
                out.append(factor * b)
            else:
                out.append(a + factor * b)
        return out

    one = jnp.ones_like(moment[0])
    resid, direc, mult = [one], [one], []
    rz_now = moment[0]
    for step in range(ITERS):
        image = [None] + direc
        alpha = rz_now / inner(direc, image)
        mult = plus(mult, alpha, direc)
        resid = plus(resid, -alpha, image)
        if step + 1 < ITERS:
            rz_new = inner(resid, resid)
            direc = plus(resid, rz_new / rz_now, direc)
            rz_now = rz_new
    return mult, resid


def finish(
    sums, right, from_next, scale, cuts, rhs_far, first_far, second_far, mult, resid,
    rhs, first, second, sems
):
    made = copies((rhs_far, first_far, second_far), (rhs, first, second), sems)
    iface = right.shape[0]
    total = sums[0]
    for i in range(1, sums.shape[0]):
        total = total + sums[i]
    mults, resids = conjugate([total[i:i + 1] for i in range(2 * ITERS)])
    for copy in made:
        copy.wait()
    u = [rhs[...], first[...], second[...], right[...] - from_next[...]]
    mult[...] = times(scale[pl.ds(0, iface), :], sum(c * v for c, v in zip(mults, u)))
    resid[...] = times(cuts[...], sum(c * v for c, v in zip(resids, u)))


def local(
    rhs_jump, incision, precond, left_rows, right_rows, diag_inv, coupling, coarse_basis, coarse_inv
):
    rhs = rhs_jump[0, 0]
    iface, width = rhs.shape
    peers = lax.axis_size("grp")
    plane, tall = (iface, width), (2 * iface, width)
    near, whole = (plane, F32), (tall, F32)
    got = passed_along(rhs, "sub", 1)
    weight = precond[0] * incision[0].astype(F32)
    weight = jnp.broadcast_to(weight, (8, iface))
    got_weight = passed_along(weight, "sub", 1)
    weights, cuts = fused(begin, (iface, 128), (iface, 128))(incision[0], precond[0])

    dinv = diag_inv[0, 0]
    coup = coupling[0, 0]
    nblk, blk = dinv.shape[0], dinv.shape[1]
    basis = coarse_basis[0, 0]
    rows = jnp.concatenate([right_rows[0, 0], left_rows[0, 0]])
    picks = [
        (lax.broadcasted_iota(jnp.int32, (blk, 2 * iface), 0) + k * blk == rows[None]).astype(F32)
        for k in range(nblk)
    ]
    sweeps = []
    for k in range(nblk):
        now = picks[k]
        if k > 0:
            now = now - jnp.dot(coup[k - 1], sweeps[-1], precision=HIGH)
        sweeps.append(jnp.dot(dinv[k], now, precision=HIGH))
    sweep = jnp.concatenate(sweeps, axis=0)
    schur = lax.dot_general(sweep, sweep, (((0,), (0,)), ((), ())), precision=HIGH)
    pick = jnp.concatenate(picks, axis=0)
    modes = lax.dot_general(pick, basis.reshape(nblk * blk, -1), (((0,), (0,)), ((), ())), precision=HIGH)
    probe = lax.dot_general(coarse_inv[0], modes, (((1,), (1,)), ((), ())), precision=FULL)
    primal = modes.shape[1]
    deal = primal // peers
    pair = (primal // 2, width)
    chips = [[i for i in range(peers) if i % 2 == core] for core in range(2)]
    swap = [(i, i ^ 1) for i in range(peers)]
    load, scale, mine, away = fused(
        enter, tall, (2 * iface, 128), pair, pair, kept=(0,), room=[whole]
    )(rhs, got, got_weight, weights, probe)
    jumps = [rhs]
    for step in range(ITERS - 1):
        (both,) = fused(paired, (peers // 2,) + pair)(mine, lax.ppermute(away, "grp", swap))
        both = exchanged(both, "grp", chips)
        (solved,) = fused(solve, tall, held=(1,), room=[whole])(schur, load)
        (mine,) = fused(summed, pair)(both)
        right, left = fused(displace_pair, plane, plane)(
            solved, modes, mine, lax.ppermute(mine, "grp", swap)
        )
        from_next = passed_along(left, "sub", -1)
        from_prev = passed_along(right, "sub", 1)
        sides = (right, left, from_next, from_prev, scale)
        if step + 2 == ITERS:
            load, jump, parts = fused(
                again_last, tall, plane, (peers, 2 * deal, width),
                kept=(0, 1), room=[whole, near],
            )(*sides, probe, modes)
        else:
            load, jump, mine, away = fused(
                again, tall, plane, pair, pair, kept=(0, 1), room=[whole, near]
            )(*sides, probe)
        jumps.append(jump)
    got = exchanged(parts, "grp")
    solved, moments = fused(
        solve_last, tall, (peers, width), held=(2, 3, 4, 5),
        room=[whole, near, near, near],
    )(schur, scale, load, *jumps)
    (spread,) = fused(added_last, (peers, deal + peers, width))(got, moments)
    gathered = exchanged(spread, "grp")

    size = lax.axis_size("sub")
    run = size // 4
    runs = [[i * run + j for j in range(run)] for i in range(4)]
    across = [[i * run + j for i in range(4)] for j in range(run)]
    (sums,) = fused(functools.partial(tally, deal), (run, 8, width))(gathered)
    sums = exchanged(sums, "sub", runs)
    right, left = fused(functools.partial(displace, deal), plane, plane)(solved, modes, gathered)
    from_next = passed_along(left, "sub", -1)
    (sums,) = fused(added, (4, 8, width))(sums)
    sums = exchanged(sums, "sub", across)
    multipliers, residual = fused(
        finish, plane, plane, held=(5, 6, 7), room=[near, near, near]
    )(sums, right, from_next, scale, cuts, *jumps)
    return (multipliers[None, None], residual[None, None])


def solution(mesh):
    placed = (
        P("sub", "grp", None, None),
        P("sub", "grp", None),
        P("sub", "grp", None),
        P("sub", "grp", None),
        P("sub", "grp", None),
        P("sub", "grp", None, None, None),
        P("sub", "grp", None, None, None),
        P("sub", "grp", None, None, None),
        P("sub", None, None),
    )

    return jax.shard_map(
        local,
        mesh=mesh,
        in_specs=placed,
        out_specs=(P("sub", "grp", None, None), P("sub", "grp", None, None)),
        check_vma=False,
    )
```
